32 devices in a mesh: tile: 8 (over z, x), beam: 4 (over y, core).
Axes of the slice: x: 2, y: 2, z: 4, core: 2. Of those that a mesh axis runs over, the one named last changes fastest.
Arguments:
- smatrix: bfloat16 [2, 2048, 512, 512], P(None, ('beam', 'tile')), may hold values from -6 to 6
- offset_y: int32 [128], replicated, may hold values from 0 to 511, as said below
- offset_x: int32 [128], replicated, may hold values from 0 to 511
- beam_qx: int32 [2048], P('beam'), may hold values from -64 to 63
- beam_qy: int32 [2048], P('beam'), may hold values from -64 to 63
- beam_amp: float32 [2048], P('beam'), may hold values from 0.5 to 2
- beam_phase: float32 [2048], P('beam'), may hold values from -3.140625 to 3.140625
Outputs:
- intensity: float32 [128, 128, 128], P(('tile', 'beam'))
The draws below stay inside these ranges and needn't reach their ends.
Inputs may be any that keep to these rules, and one draw needn't show every extreme that they name: `offset_y`: the window of position p starts in field rows 64 * (p // 16) to 64 * (p // 16) + 63.
All inputs are finite; a program needn't handle non-finite values.
Results may differ from the reference program's by a relative error of at most 0.017.
Values may be sent and summed in bfloat16 or wider, within the bound.
No kernel may reach another device: no remote copies, remote signals or barrier semaphores. Data moves between devices by JAX's collectives and lax.ppermute only.
A program may use at most 256 MiB of HBM per device.

```python
import math
import jax
import jax.numpy as jnp
from jax import lax

BEAMS = 2048
CROP = 128
POS_DEV = 16
FIELD = 512
POSITIONS = 128
STRIP = 64
N_BEAM = 4


def draw_offset_y(key, part):
    places = jnp.arange(POSITIONS, dtype=jnp.int32)
    start = places // POS_DEV * STRIP
    jitter = jax.random.randint(key, (POSITIONS,), 0, STRIP, dtype=jnp.int32)
    slot = places % POS_DEV
    jitter = jnp.where(slot == 0, STRIP - 1, jnp.where(slot == 1, 0, jitter))
    return (start + jitter).astype(jnp.int32)


def with_ends(result, key, low, largest):
    shape = result.shape
    index_at = [jax.random.randint(jax.random.fold_in(key, axis), (), 0, shape[axis]) for axis in range(len(shape))]
    result = result.at[tuple(index_at)].set(low)
    longest = shape.index(max(shape))
    index_at[longest] = (index_at[longest] + 1) % shape[longest]
    return result.at[tuple(index_at)].set(largest)


def level_of(own_key, shape, pieces, smallest, top_value):
    loudness, own = 1.0, jax.random.fold_in(own_key, 6)
    for position, parts in pieces:
        draws = jnp.exp(jax.random.uniform(jax.random.fold_in(own, position), (parts,), jnp.float32, smallest / len(pieces), top_value / len(pieces)))
        loudness = loudness * jnp.repeat(draws, shape[position] // parts).reshape([-1 if axis == position else 1 for axis in range(len(shape))])
    return loudness


def normal_values(key, dims, spread, most, shards=(), held_as=jnp.bfloat16):
    drawn = spread * jax.random.normal(key, dims, jnp.float32)
    if shards:
        drawn = drawn * level_of(key, dims, shards, -0.22, 0.18)
    return jnp.clip(drawn, -most, most).astype(held_as)


def setup_inputs(seed: int = 0) -> dict:
    key_list = jax.random.split(jax.random.key(seed), 8)
    smatrix = normal_values(key_list[0], (2, BEAMS, FIELD, FIELD), 1.0, 6.0, ((1, 32),))
    offset_y = draw_offset_y(jax.random.fold_in(key_list[7], 71), 0)
    offset_x = with_ends(jax.random.randint(key_list[2], (POSITIONS,), 0, FIELD), jax.random.fold_in(key_list[2], 1), 0, FIELD - 1).astype(jnp.int32)
    beam_qx = with_ends(jax.random.randint(key_list[3], (BEAMS,), 0 - FIELD // 8, FIELD // 8), jax.random.fold_in(key_list[3], 1), 0 - FIELD // 8, (FIELD // 8) - 1).astype(jnp.int32)
    beam_qy = with_ends(jax.random.randint(key_list[4], (BEAMS,), 0 - FIELD // 8, FIELD // 8), jax.random.fold_in(key_list[4], 1), 0 - FIELD // 8, (FIELD // 8) - 1).astype(jnp.int32)
    beam_amp = jnp.clip(jnp.exp(math.log(2.0) - 1.3862944 * jax.random.uniform(key_list[5], (BEAMS,), jnp.float32) ** level_of(key_list[5], (BEAMS,), ((0, 4),), -0.2, 0.2)), 0.5, 2.0)
    beam_phase = jnp.clip(jax.random.uniform(key_list[6], (BEAMS,), jnp.float32, -3.140625, 3.140625), -3.140625, 3.140625)
    return {"smatrix": smatrix, "offset_y": offset_y, "offset_x": offset_x, "beam_qx": beam_qx, "beam_qy": beam_qy, "beam_amp": beam_amp, "beam_phase": beam_phase}


two_pi = 2.0 * math.pi

def reference(smatrix, offset_y, offset_x, beam_qx, beam_qy, beam_amp, beam_phase):
    group_beams = BEAMS // N_BEAM
    scale = beam_amp * (1.0 / math.sqrt(BEAMS))
    places = jnp.arange(CROP, dtype=jnp.int32)

    def one_position(pair):
        first_y, first_x = pair
        turns = ((first_x + CROP // 2) * beam_qx + (first_y + CROP // 2) * beam_qy) % FIELD
        angle = beam_phase - two_pi * turns.astype(jnp.float32) / FIELD
        w_real = lax.optimization_barrier((scale * jnp.cos(angle)).astype(jnp.bfloat16)).astype(jnp.float32)
        w_imag = lax.optimization_barrier((scale * jnp.sin(angle)).astype(jnp.bfloat16)).astype(jnp.float32)
        w_real = w_real.reshape(N_BEAM, group_beams)
        w_imag = w_imag.reshape(N_BEAM, group_beams)
        rows = ((first_y + places) % FIELD).astype(jnp.int32)
        cols = ((first_x + places) % FIELD).astype(jnp.int32)
        window = jnp.take(jnp.take(smatrix, rows, axis=2), cols, axis=3)
        window = window.astype(jnp.float32).reshape(2, N_BEAM, group_beams, CROP, CROP)
        part_re = jnp.einsum('gb,gbij->gij', w_real, window[0]) - jnp.einsum('gb,gbij->gij', w_imag, window[1])
        part_im = jnp.einsum('gb,gbij->gij', w_real, window[1]) + jnp.einsum('gb,gbij->gij', w_imag, window[0])
        part_re = lax.optimization_barrier(part_re.astype(jnp.bfloat16)).astype(jnp.float32)
        part_im = lax.optimization_barrier(part_im.astype(jnp.bfloat16)).astype(jnp.float32)
        exit_re = lax.optimization_barrier(jnp.sum(part_re, axis=0))
        exit_im = lax.optimization_barrier(jnp.sum(part_im, axis=0))
        spectrum = jnp.fft.fft2(exit_re + 1j * exit_im) / CROP
        return (spectrum.real * spectrum.real + spectrum.imag * spectrum.imag).astype(jnp.float32)
    return lax.map(one_position, (offset_y, offset_x))
```

```python
import functools
import math

import jax
import jax.numpy as jnp
from jax import lax
from jax.experimental import pallas as pl
from jax.experimental.pallas import tpu as pltpu
from jax.sharding import PartitionSpec as P

BEAMS = 2048
CROP = 128
POS_DEV = 16
ROWS = 8
CHUNKS = 4

two_pi = 2.0 * math.pi


def exchanged(value, axis, bit):
    count = lax.axis_size(axis)
    return lax.ppermute(value, axis, [(i, i ^ bit) for i in range(count)])


def waves_kernel(
    tiles, beams, first_step, tile_ref, s_ref, w_ref, block_ref, low_ref, keep_ref, send_ref, rows_ref
):
    planes, group, turns, _, field = s_ref.shape
    depth = planes * group
    strip = field // tiles
    reach = CROP // strip
    per_owner = 2 * POS_DEV
    base_row = (pl.program_id(0) + first_step) * ROWS
    strip_at = base_row // strip
    row_in_strip = base_row % strip
    own_tile = tile_ref[0]
    half = per_owner // 2
    groups = field // CROP

    for k in range(turns):
        for c in range(groups):
            piece = s_ref[:, :, k, :, c * CROP : (c + 1) * CROP].astype(jnp.float32)
            rows_ref[k, c] = piece.reshape(depth * ROWS, CROP)

    def one_row(r, carry):
        late = None
        first = None
        for k in range(turns):
            start = pl.multiple_of((reach * k + strip_at) * per_owner, per_owner)
            count = (reach + 1) * per_owner
            values = [
                rows_ref[k, c, pl.ds(r, depth, stride=ROWS), :].astype(jnp.bfloat16)
                for c in range(groups)
            ]
            values = jnp.concatenate(values, axis=1)
            out = jnp.dot(
                w_ref[pl.ds(start, count), :], values, preferred_element_type=jnp.float32
            )
            block = block_ref[pl.ds(start, count), :]
            folded = out[:, (groups - 1) * CROP :]
            for c in range(groups - 1):
                folded = jnp.where(block == c, out[:, c * CROP : (c + 1) * CROP], folded)
            low = low_ref[pl.ds(start, per_owner), :]
            yield_k = (folded, low)
            if k == 0:
                first = yield_k
            else:
                store(r, k, late, yield_k)
            late = folded
        store(r, turns, late, first)
        return carry

    def store(r, k, before, here):
        folded, low = here
        for e in range(reach):
            owner = (reach * (k - 1) + strip_at + e) % tiles
            part = folded[e * per_owner : (e + 1) * per_owner]
            if e == 0:
                began = before[reach * per_owner :]
                part = jnp.where(low <= row_in_strip + r, began, part)
            part = part.astype(jnp.bfloat16)
            place = owner ^ own_tile
            keep_ref[r, place] = part[:half]
            send_ref[r, place] = part[half:]

    for r in range(ROWS):
        one_row(r, 0)


def partial_waves(chunk, smatrix, own_tile, weights, block, low):
    planes, group, field, _ = smatrix.shape
    tiles = lax.axis_size("tile")
    beams = lax.axis_size("beam")
    rows = CROP // CHUNKS
    steps = rows // ROWS
    turns = field // CROP
    viewed = smatrix.reshape(planes, group, turns, CROP, field)
    half = POS_DEV
    shape = jax.ShapeDtypeStruct((rows, tiles, half, CROP), jnp.bfloat16)
    out_spec = pl.BlockSpec((ROWS, tiles, half, CROP), lambda i, t: (i, 0, 0, 0))
    whole = pl.BlockSpec(memory_space=pltpu.VMEM)
    first_step = chunk * steps
    flops = 2 * 3 * 2 * POS_DEV * planes * group * field * field // CHUNKS
    return pl.pallas_call(
        functools.partial(waves_kernel, tiles, beams, first_step),
        out_shape=(shape, shape),
        grid_spec=pltpu.PrefetchScalarGridSpec(
            num_scalar_prefetch=1,
            grid=(steps,),
            in_specs=[
                pl.BlockSpec(
                    (planes, group, turns, ROWS, field), lambda i, t: (0, 0, 0, i + first_step, 0)
                ),
                whole,
                whole,
                whole,
            ],
            out_specs=(out_spec, out_spec),
            scratch_shapes=[
                pltpu.VMEM((turns, field // CROP, planes * group * ROWS, CROP), jnp.float32)
            ],
        ),
        compiler_params=pltpu.CompilerParams(vmem_limit_bytes=48 * 1024 * 1024),
        cost_estimate=pl.CostEstimate(
            flops=flops,
            bytes_accessed=smatrix.size * 2 // CHUNKS,
            transcendentals=0,
        ),
        name=f"waves_{chunk}",
    )(own_tile, viewed, weights, block, low)


def intensity_kernel(share, wave_ref, right_ref, left_ref, out_ref, rows_ref):
    rows_ref[...] = wave_ref[...].reshape(CROP * 2 * share, CROP)
    for q in range(share):
        real = rows_ref[pl.ds(2 * q, CROP, stride=2 * share), :]
        imag = rows_ref[pl.ds(2 * q + 1, CROP, stride=2 * share), :]
        joined = jnp.concatenate([real, imag], axis=1)
        halves = jnp.dot(
            joined, right_ref[...], precision=lax.Precision.HIGHEST,
            preferred_element_type=jnp.float32,
        )
        halves = jnp.concatenate([halves[:, :CROP], halves[:, CROP:]], axis=0)
        full = jnp.dot(
            left_ref[...], halves, precision=lax.Precision.HIGHEST,
            preferred_element_type=jnp.float32,
        )
        full_re, full_im = full[:CROP], full[CROP:]
        out_ref[q] = full_re * full_re + full_im * full_im


def intensities(waves):
    share = waves.shape[1] // 2
    places = jnp.arange(CROP, dtype=jnp.int32)
    ticks = places[:, None] * places[None, :] % CROP
    angle = two_pi * ticks.astype(jnp.float32) / CROP
    norm_factor = 1.0 / math.sqrt(CROP)
    table_re = jnp.cos(angle) * norm_factor
    table_im = -jnp.sin(angle) * norm_factor
    right = jnp.concatenate(
        [
            jnp.concatenate([table_re, table_im], axis=1),
            jnp.concatenate([-table_im, table_re], axis=1),
        ],
        axis=0,
    )
    left = jnp.concatenate(
        [
            jnp.concatenate([table_re, -table_im], axis=1),
            jnp.concatenate([table_im, table_re], axis=1),
        ],
        axis=0,
    )
    return pl.pallas_call(
        functools.partial(intensity_kernel, share),
        out_shape=jax.ShapeDtypeStruct((share, CROP, CROP), jnp.float32),
        in_specs=[pl.BlockSpec(memory_space=pltpu.VMEM)] * 3,
        out_specs=pl.BlockSpec(memory_space=pltpu.VMEM),
        scratch_shapes=[pltpu.VMEM((CROP * 2 * share, CROP), jnp.float32)],
        name="intensity",
    )(waves, right, left)


def local(smatrix, offset_y, offset_x, beam_qx, beam_qy, beam_amp, beam_phase):
    tiles = lax.axis_size("tile")
    beams = lax.axis_size("beam")
    own_tile = lax.axis_index("tile")
    own_group = lax.axis_index("beam")
    planes, group, field, _ = smatrix.shape
    strip = field // tiles
    reach = CROP // strip
    share = POS_DEV // beams

    places = jnp.arange(beams, dtype=jnp.int32)
    order = (places % (beams // 2) * 2 + places // (beams // 2)) ^ own_group
    first_y = offset_y.reshape(tiles, beams, share)[:, order].reshape(tiles * POS_DEV)
    first_x = offset_x.reshape(tiles, beams, share)[:, order].reshape(tiles * POS_DEV)
    begin = own_tile * group
    qx = lax.dynamic_slice_in_dim(beam_qx, begin, group)
    qy = lax.dynamic_slice_in_dim(beam_qy, begin, group)
    amp = lax.dynamic_slice_in_dim(beam_amp, begin, group)
    phase = lax.dynamic_slice_in_dim(beam_phase, begin, group)
    scale = amp * (1.0 / math.sqrt(BEAMS))
    turns = (
        (first_x + CROP // 2)[:, None] * qx[None, :]
        + (first_y + CROP // 2)[:, None] * qy[None, :]
    ) % field
    angle = phase[None, :] - two_pi * turns.astype(jnp.float32) / field
    w_real = (scale[None, :] * jnp.cos(angle)).astype(jnp.bfloat16)
    w_imag = (scale[None, :] * jnp.sin(angle)).astype(jnp.bfloat16)
    real_row = jnp.concatenate([w_real, -w_imag], axis=1)
    imag_row = jnp.concatenate([w_imag, w_real], axis=1)
    weights = jnp.stack([real_row, imag_row], axis=1).reshape(tiles * 2 * POS_DEV, planes * group)
    lanes = jnp.arange(CROP, dtype=jnp.int32)
    wraps = (first_x % field // CROP)[:, None] + (lanes[None, :] < (first_x % CROP)[:, None])
    block = jnp.repeat(wraps % (field // CROP), 2, axis=0).astype(jnp.int32)
    low = jnp.broadcast_to(jnp.repeat(first_y % strip, 2)[:, None], block.shape).astype(jnp.int32)

    def wrapped(table):
        return jnp.concatenate([table[-reach * 2 * POS_DEV :], table], axis=0)

    weights, block, low = wrapped(weights), wrapped(block), wrapped(low)
    own = own_tile.reshape(1).astype(jnp.int32)

    tile_bits = [1 << b for b in range(tiles.bit_length() - 1)]
    beam_bits = [1 << b for b in range(beams.bit_length() - 1)]
    plain = [("beam", b) for b in beam_bits[:0:-1]]
    pieces = []
    for chunk in range(CHUNKS):
        keep, send = partial_waves(chunk, smatrix, own, weights, block, low)
        pieces.append(reduce_chunk(keep, send, chunk, tile_bits, beam_bits, share))
    waves = jnp.concatenate(pieces, axis=0)
    return intensities(waves)


def reduce_chunk(keep, send, chunk, tile_bits, beam_bits, share):
    rows = keep.shape[0]
    arrived = exchanged(send, "beam", 1)
    names = [("tile", b) for b in reversed(tile_bits)]
    names += [("beam", b) for b in reversed(beam_bits[1:])]
    shape = (rows,) + (2,) * len(names) + (2 * share, CROP)
    terms = [keep.reshape(shape), arrived.reshape(shape)]
    first_tile = [("tile", tile_bits[0])]
    rest_tile = [("tile", b) for b in tile_bits[1:]]
    rest_beam = [("beam", b) for b in beam_bits[1:]]
    plan = first_tile + rest_beam if chunk % 2 == 0 else rest_beam + first_tile
    for name in plan + rest_tile:
        at = 1 + names.index(name)
        names.remove(name)
        away = [lax.index_in_dim(t, 1, at, keepdims=False).astype(jnp.float32) for t in terms]
        stay = [lax.index_in_dim(t, 0, at, keepdims=False) for t in terms]
        packed = functools.reduce(jnp.add, away).astype(jnp.bfloat16)
        terms = stay + [exchanged(packed, *name)]
    total = functools.reduce(jnp.add, [t.astype(jnp.float32) for t in terms])
    return total.reshape(rows, 2 * share, CROP)


def solution(mesh):
    return jax.shard_map(
        local,
        mesh=mesh,
        in_specs=(
            P(None, ("beam", "tile"), None, None),
            P(),
            P(),
            P("beam"),
            P("beam"),
            P("beam"),
            P("beam"),
        ),
        out_specs=P(("tile", "beam"), None, None),
        check_vma=False,
    )
```

```python
import functools
import math

import jax
import jax.numpy as jnp
import numpy as np
from jax import lax
from jax.experimental import pallas as pl
from jax.experimental.pallas import tpu as pltpu
from jax.sharding import PartitionSpec as P


BEAMS = 2048
CROP = 128
POS_DEV = 16
ROWS = 8
CHUNKS = (32, 32, 32, 32)
FIRST = "xyxy"

two_pi = 2.0 * math.pi


def exchanged(value, axis, bit):
    count = lax.axis_size(axis)
    return lax.ppermute(value, axis, [(i, i ^ bit) for i in range(count)])


def waves_kernel(tiles, beams, groups, plan, first_step, tile_ref, *refs):
    s_refs = refs[: groups * groups]
    w_ref, block_ref, low_ref, keep_ref, send_ref, rows_ref, edge_ref = refs[groups * groups :]
    strip = groups * CROP // tiles
    reach = CROP // strip
    per_owner = 2 * POS_DEV
    base_row = (pl.program_id(0) + first_step) * ROWS
    strip_at = base_row // strip
    row_in_strip = base_row % strip
    turns = groups
    own_tile = tile_ref[0]
    half = per_owner // 2
    piece = per_owner // beams
    count = (reach + 1) * per_owner

    def destinations(owner):
        place = (owner % tiles) ^ own_tile
        found = []
        for j in range(beams // 2):
            index = 0
            for axis, bit in plan:
                on = (place // bit) % 2 if axis == "tile" else j // (bit // 2) % 2
                index = 2 * index + on
            found.append(index)
        return found

    def store(r, found, part):
        part = part.astype(jnp.bfloat16)
        for j, index in enumerate(found):
            keep_ref[index, r] = part[j * piece : (j + 1) * piece]
            send_ref[index, r] = part[half + j * piece : half + (j + 1) * piece]

    def store_edge(r, found, start, began, ended):
        low = low_ref[pl.ds(start, per_owner), :]
        store(r, found, jnp.where(low <= row_in_strip + r, began, ended))

    for k in range(turns):
        for c in range(groups):
            rows_ref[k, c] = jnp.swapaxes(s_refs[k * groups + c][...], 0, 1)
        start = pl.multiple_of((reach * k + strip_at) * per_owner, per_owner)
        found = [destinations(reach * (k - 1) + strip_at + e) for e in range(reach)]
        for r in range(ROWS):
            values = jnp.concatenate([rows_ref[k, c, r] for c in range(groups)], axis=1)
            out = jnp.dot(
                w_ref[pl.ds(start, count), :], values, preferred_element_type=jnp.float32
            )
            block = block_ref[pl.ds(start, count), :]
            folded = out[:, (groups - 1) * CROP :]
            for c in range(groups - 1):
                folded = jnp.where(block == c, out[:, c * CROP : (c + 1) * CROP], folded)
            for e in range(1, reach):
                store(r, found[e], folded[e * per_owner : (e + 1) * per_owner])
            if k == 0:
                edge_ref[0, r] = folded[:per_owner]
            else:
                store_edge(r, found[0], start, edge_ref[1, r], folded[:per_owner])
            edge_ref[1, r] = folded[reach * per_owner :]
    found = destinations(reach * (turns - 1) + strip_at)
    for r in range(ROWS):
        first = pl.multiple_of(strip_at * per_owner, per_owner)
        store_edge(r, found, first, edge_ref[1, r], edge_ref[0, r])


def partial_waves(chunk, plan, smatrix, own_tile, weights, block, low):
    planes, group, field, _ = smatrix.shape
    tiles = lax.axis_size("tile")
    rows = CHUNKS[chunk]
    steps = rows // ROWS
    turns = field // CROP
    viewed = smatrix.reshape(planes * group, field, field)
    beams = lax.axis_size("beam")
    places = tiles * beams // 2
    piece = 2 * POS_DEV // beams
    shape = jax.ShapeDtypeStruct((places, rows, piece, CROP), jnp.bfloat16)
    out_spec = pl.BlockSpec((places, ROWS, piece, CROP), lambda i, t: (0, i, 0, 0))
    whole = pl.BlockSpec(memory_space=pltpu.VMEM)
    first_step = sum(CHUNKS[:chunk]) // ROWS
    flops = 2 * 3 * 2 * POS_DEV * planes * group * field * field * rows // CROP
    return pl.pallas_call(
        functools.partial(waves_kernel, tiles, beams, turns, plan, first_step),
        out_shape=(shape, shape),
        grid_spec=pltpu.PrefetchScalarGridSpec(
            num_scalar_prefetch=1,
            grid=(steps,),
            in_specs=[
                *[
                    pl.BlockSpec(
                        (planes * group, ROWS, CROP),
                        functools.partial(lambda k, c, i, t: (0, k * (CROP // ROWS) + i + first_step, c), k, c),
                    )
                    for k in range(turns)
                    for c in range(turns)
                ],
                whole,
                whole,
                whole,
            ],
            out_specs=(out_spec, out_spec),
            scratch_shapes=[
                pltpu.VMEM((turns, turns, ROWS, planes * group, CROP), jnp.bfloat16),
                pltpu.VMEM((2, ROWS, 2 * POS_DEV, CROP), jnp.float32),
            ],
        ),
        compiler_params=pltpu.CompilerParams(vmem_limit_bytes=48 * 1024 * 1024),
        cost_estimate=pl.CostEstimate(
            flops=flops,
            bytes_accessed=smatrix.size * 2 * rows // CROP,
            transcendentals=0,
        ),
    )(own_tile, *[viewed] * (turns * turns), weights, block, low)


def halves_of(value):
    high = value.astype(jnp.bfloat16)
    return high, (value - high.astype(jnp.float32)).astype(jnp.bfloat16)


def split_dot(a, b):
    dot = functools.partial(jnp.dot, preferred_element_type=jnp.float32)
    return dot(a[0], b[0]) + (dot(a[0], b[1]) + dot(a[1], b[0]))


def intensity_kernel(share, counts, right_ref, left_ref, *refs):
    *wave_refs, out_ref, rows_ref = refs
    begin = 0
    for count in counts:
        terms = [wave_refs.pop(0)[0].astype(jnp.float32) for _ in range(count)]
        total = functools.reduce(jnp.add, terms)
        size = total.shape[0] * 2 * share
        rows_ref[pl.ds(begin, size), :] = total.reshape(size, CROP)
        begin += size
    right, left = halves_of(right_ref[...]), halves_of(left_ref[...])
    begin = 0
    for wave_ref in wave_refs:
        size = wave_ref.shape[0] * 2 * share
        rows_ref[pl.ds(begin, size), :] = wave_ref[...].reshape(size, CROP)
        begin += size
    for q in range(share):
        real = rows_ref[pl.ds(2 * q, CROP, stride=2 * share), :]
        imag = rows_ref[pl.ds(2 * q + 1, CROP, stride=2 * share), :]
        joined = jnp.concatenate([real, imag], axis=1)
        halves = split_dot(halves_of(joined), right)
        halves = jnp.concatenate([halves[:, :CROP], halves[:, CROP:]], axis=0)
        full = split_dot(left, halves_of(halves))
        full_re, full_im = full[:CROP], full[CROP:]
        out_ref[q] = full_re * full_re + full_im * full_im


def intensities(sums, share):
    counts = tuple(len(terms) for terms in sums)
    waves = [term for terms in sums for term in terms]
    places = np.arange(CROP)
    angle = two_pi * (places[:, None] * places[None, :] % CROP) / CROP
    table_re = np.cos(angle) / math.sqrt(CROP)
    table_im = -np.sin(angle) / math.sqrt(CROP)
    right = np.block([[table_re, table_im], [-table_im, table_re]]).astype(np.float32)
    left = np.block([[table_re, -table_im], [table_im, table_re]]).astype(np.float32)
    return pl.pallas_call(
        functools.partial(intensity_kernel, share, counts),
        out_shape=jax.ShapeDtypeStruct((share, CROP, CROP), jnp.float32),
        grid=(1,),
        in_specs=[pl.BlockSpec((2 * CROP, 2 * CROP), lambda i: (0, 0))] * 2
        + [
            pl.BlockSpec(
                (1, rows, t.shape[2], CROP), functools.partial(lambda at, i: (0, at, 0, 0), begin // rows)
            )
            for t, begin, rows in waves
        ],
        out_specs=pl.BlockSpec((share, CROP, CROP), lambda i: (0, 0, 0)),
        scratch_shapes=[pltpu.VMEM((CROP * 2 * share, CROP), jnp.float32)],
        name="intensity",
    )(right, left, *[t for t, _, _ in waves])


def local(smatrix, offset_y, offset_x, beam_qx, beam_qy, beam_amp, beam_phase):
    tiles = lax.axis_size("tile")
    beams = lax.axis_size("beam")
    own_tile = lax.axis_index("tile")
    own_group = lax.axis_index("beam")
    planes, group, field, _ = smatrix.shape
    strip = field // tiles
    reach = CROP // strip
    share = POS_DEV // beams

    per_owner = 2 * POS_DEV
    row = jnp.arange((tiles + reach) * per_owner, dtype=jnp.int32)
    place = row % per_owner // (2 * share)
    target = (place % (beams // 2) * 2 + place // (beams // 2)) ^ own_group
    owner = (row // per_owner + tiles - reach) % tiles
    position = (owner * beams + target) * share + row // 2 % share
    listed = jnp.arange(offset_y.shape[0], dtype=jnp.int32)
    hit = position[:, None] == listed[None, :]
    first_y = jnp.sum(jnp.where(hit, offset_y[None, :], 0), axis=1, dtype=jnp.int32)[:, None]
    first_x = jnp.sum(jnp.where(hit, offset_x[None, :], 0), axis=1, dtype=jnp.int32)[:, None]

    table = jnp.stack(
        [beam_qx.astype(jnp.float32), beam_qy.astype(jnp.float32), beam_amp, beam_phase]
    )
    table = lax.dynamic_slice_in_dim(table, own_tile * group, group, 1)
    table = jnp.concatenate([table, table], axis=1)
    qx, qy = table[0:1].astype(jnp.int32), table[1:2].astype(jnp.int32)
    scale = table[2:3] * (1.0 / math.sqrt(BEAMS))
    turns = ((first_x + CROP // 2) * qx + (first_y + CROP // 2) * qy) % field
    angle = table[3:4] - two_pi * turns.astype(jnp.float32) / field
    w_real, w_imag = scale * jnp.cos(angle), scale * jnp.sin(angle)
    imag_out = (row % 2 == 1)[:, None]
    imag_in = (jnp.arange(planes * group, dtype=jnp.int32) >= group)[None, :]
    weights = jnp.where(
        imag_out == imag_in, w_real, jnp.where(imag_out, w_imag, -w_imag)
    ).astype(jnp.bfloat16)
    lanes = jnp.arange(CROP, dtype=jnp.int32)[None, :]
    block = (first_x // CROP + (lanes < first_x % CROP).astype(jnp.int32)) % (field // CROP)
    low = jnp.broadcast_to(first_y % strip, block.shape)
    own = own_tile.reshape(1).astype(jnp.int32)

    tile_bits = [1 << b for b in range(tiles.bit_length() - 1)]
    beam_bits = [1 << b for b in range(beams.bit_length() - 1)]
    near = [("tile", tile_bits[0])]
    rest = [("tile", b) for b in tile_bits[1:]]
    beside = [("beam", b) for b in beam_bits[1:]]
    sums = []
    for chunk in range(len(CHUNKS)):
        plan = near + beside if FIRST[chunk] == "x" else beside + near
        keep, send = partial_waves(
            chunk, tuple(plan + rest), smatrix, own, weights, block, low
        )
        arrived = exchanged(send, "beam", 1)
        rows = CHUNKS[chunk]
        terms = [(keep, 0, rows), (arrived, 0, rows)]
        count = keep.shape[0]
        for name in plan:
            count //= 2
            terms = halved([terms], name, count)[0]
        sums.append(terms)
    for first in range(len(CHUNKS)):
        pair = sums[first : first + 1]
        left = count
        for name in rest:
            left //= 2
            pair = halved(pair, name, left)
        sums[first : first + 1] = pair
    return intensities(sums, share)


def halved(sums, name, count):
    packed = []
    for terms in sums:
        away = [
            t[count : 2 * count, begin : begin + rows].astype(jnp.float32)
            for t, begin, rows in terms
        ]
        packed.append(functools.reduce(jnp.add, away).astype(jnp.bfloat16))
    packed = packed[0] if len(packed) == 1 else jnp.concatenate(packed, axis=1)
    arrived = exchanged(packed, *name)
    result, begin = [], 0
    for terms in sums:
        rows = terms[0][2]
        result.append(terms + [(arrived, begin, rows)])
        begin += rows
    return result


def solution(mesh):
    return jax.shard_map(
        local,
        mesh=mesh,
        in_specs=(
            P(None, ("beam", "tile"), None, None),
            P(),
            P(),
            P("beam"),
            P("beam"),
            P("beam"),
            P("beam"),
        ),
        out_specs=P(("tile", "beam"), None, None),
        check_vma=False,
    )
```
